32 devices in a mesh: dish: 4 (over y, x), chan: 8 (over z, core).
Axes of the slice: x: 2, y: 2, z: 4, core: 2. Of those that a mesh axis runs over, the one named last changes fastest.
Arguments:
- voltages: bfloat16 [2, 64, 4096, 512], P(None, 'dish', 'chan'), may hold values from -150 to 150
- beam_weights: bfloat16 [2, 4096, 64, 1024], P(None, ('chan', 'dish')), may hold values from -0.5 to 0.5
- flags: int32 [4096], P('chan'), may hold values 0 or 1
- sk_bins: int32 [4096], P('chan'), may hold values from 1 to 8
- bin_of_sample: int32 [512], replicated, may hold values from 0 to 63, never falling along the last dimension, each value on 1 to 16 neighbouring positions
Outputs:
- beam_power: bfloat16 [4096, 65536], P(None, ('dish', 'chan'))
The draws below stay inside these ranges and needn't reach their ends.
Inputs may be any that keep to these rules, and one draw needn't show every extreme that they name: `bin_of_sample`: never falls; each of the 64 bins holds 1 to 16 samples.
All inputs are finite; a program needn't handle non-finite values. No bound on the sum of `flags` on one device may be relied on, other than what follows from the above.
Results may differ from the reference program's by a relative error of at most 0.006.
Values may be sent and summed in bfloat16 or wider, within the bound.
A program may use at most 192 MiB of HBM per device.

```python
import math
import jax
import jax.numpy as jnp
import numpy as np
from jax import lax

DISH = 64
CH = 4096
BEAMS = 1024
T_SIZE = 512
TBINS = 64


def draw_voltages(key, part):
    keys = jax.random.split(key, 4)
    base = jnp.clip(jax.random.normal(keys[0], (2, DISH, CH, T_SIZE), jnp.float32), -6.0, 6.0)
    ramped = 1.0 + 0.8 * jnp.arange(DISH, dtype=jnp.float32) / (DISH - 1)
    jitter = jnp.exp(jax.random.uniform(keys[1], (DISH,), jnp.float32, -0.15, 0.15))
    amplitude = ramped * jitter
    depth = jax.random.uniform(keys[2], (CH,), jnp.float32, 0.0, 0.35)
    swing = jnp.clip(jax.random.normal(keys[3], (CH, T_SIZE), jnp.float32), -4.0, 4.0)
    envelope = jnp.exp(depth[:, None] * swing)
    return (base * amplitude[None, :, None, None] * envelope[None, None]).astype(jnp.bfloat16)


def set_ends(values, own_key, smallest, top_value):
    index_at = [jax.random.randint(jax.random.fold_in(own_key, axis), (), 0, length) for axis, length in enumerate(values.shape)]
    widest = values.shape.index(max(values.shape))
    next_to = index_at[:widest] + [(index_at[widest] + 1) % values.shape[widest]] + index_at[widest + 1:]
    return values.at[tuple(index_at)].set(smallest).at[tuple(next_to)].set(top_value)


def shard_levels(own_key, extent, shards, smallest, top_value):
    gain = 1.0
    for axis_at, parts in shards:
        steps = jax.random.uniform(jax.random.fold_in(jax.random.fold_in(own_key, 6), axis_at), (parts,), jnp.float32, smallest / len(shards), top_value / len(shards))
        gain = gain * jnp.repeat(jnp.exp(steps), extent[axis_at] // parts).reshape((-1,) + (1,) * (len(extent) - 1 - axis_at))
    return gain


def length_profile(amount, total, most, slope):
    loads = [(1 << 20) // math.isqrt(standing ** slope) + 1 for standing in range(2, amount + 1)]
    surplus, given = total - most - (amount - 1), [1] * (amount - 1)
    while surplus > 0:
        movable = [i for i in range(amount - 1) if given[i] < most]
        mass, budget = sum([loads[i] for i in movable]), surplus
        for i in movable:
            extra = min(most - given[i], max(1, budget * loads[i] // mass), surplus)
            given[i] = given[i] + extra
            surplus = surplus - extra
    return np.array([most] + given)


def ragged(rng, count, total, reach, skew):
    if count == 2:
        one = jax.random.randint(rng, (), max(1, total - reach), min(reach, total - 1) + 1)
        return jnp.stack([one, total - one])
    lengths = jnp.asarray(length_profile(count, total, reach, skew), jnp.int32)
    pairs = (count - 1) // 2
    source_of, receiver = lengths[1:1 + 2 * pairs:2], lengths[2:2 + 2 * pairs:2]
    margin = jnp.minimum(source_of - 1, reach - receiver)
    moved = jax.random.randint(jax.random.fold_in(rng, 1), (pairs,), 0, 1 << 20) % (margin + 1)
    lengths = lengths.at[1:1 + 2 * pairs:2].set(source_of - moved).at[2:2 + 2 * pairs:2].set(receiver + moved)
    return lengths[jax.random.permutation(jax.random.fold_in(rng, 2), count)]


def gaussian(rng, shape, width, limit, pieces=(), held_as=jnp.bfloat16):
    result = width * jax.random.normal(rng, shape, jnp.float32)
    if pieces:
        result = result * shard_levels(rng, shape, pieces, -0.22, 0.18)
    return jnp.clip(result, -limit, limit).astype(held_as)


def setup_inputs(seed: int = 0) -> dict:
    seeds = jax.random.split(jax.random.key(seed), 6)
    return {
        "voltages": draw_voltages(jax.random.fold_in(seeds[5], 71), 0),
        "beam_weights": gaussian(seeds[1], (2, CH, DISH, BEAMS), (2 * DISH) ** -0.5, 0.5, ((1, 32),)),
        "flags": set_ends((jax.random.randint(seeds[2], (CH,), 0, 8) < 7).astype(jnp.int32), jax.random.fold_in(seeds[2], 1), 0, 1),
        "sk_bins": set_ends(jax.random.randint(seeds[3], (CH,), 1, 9), jax.random.fold_in(seeds[3], 1), 1, 8).astype(jnp.int32),
        "bin_of_sample": jnp.searchsorted(jnp.cumsum(ragged(seeds[4], TBINS, T_SIZE, 16, 1)), jnp.arange(T_SIZE), side="right").astype(jnp.int32),
    }


def kurtosis_scale(first_sum, second_sum, samples, flags, sk_bins):
    widths = 0.05 * sk_bins.astype(jnp.float32)
    mean_one = first_sum / samples
    mean_two = second_sum / samples
    ratio = mean_two / (mean_one * mean_one + 1e-6)
    kurtosis = (samples + 1.0) / (samples - 1.0) * (ratio - 1.0)
    excess = kurtosis - 1.0
    return flags.astype(jnp.float32) * widths / (widths + excess * excess)


def channel_average(volts, weights, onehot, counts):
    stacked_v = jnp.concatenate([volts[0], volts[1]], axis=0)
    real_rows = jnp.concatenate([weights[0], -weights[1]], axis=0)
    imag_rows = jnp.concatenate([weights[1], weights[0]], axis=0)
    stacked_w = jnp.concatenate([real_rows, imag_rows], axis=1)
    beam_volts = jnp.dot(stacked_w.T, stacked_v, preferred_element_type=jnp.float32)
    half = weights.shape[2]
    real_part = beam_volts[:half]
    imag_part = beam_volts[half:]
    powers = real_part * real_part + imag_part * imag_part
    upper = powers.astype(jnp.bfloat16)
    lower = (powers - upper.astype(jnp.float32)).astype(jnp.bfloat16)
    summed = jnp.dot(upper, onehot, preferred_element_type=jnp.float32) + jnp.dot(lower, onehot, preferred_element_type=jnp.float32)
    return summed / counts[None, :]


def reference(voltages, beam_weights, flags, sk_bins, bin_of_sample):
    floats = voltages.astype(jnp.float32)
    powers = floats[0] * floats[0] + floats[1] * floats[1]
    first_sum = jnp.sum(powers, axis=(0, 2))
    second_sum = jnp.sum(powers * powers, axis=(0, 2))
    samples = float(DISH * T_SIZE)
    scaling = kurtosis_scale(first_sum, second_sum, samples, flags, sk_bins)
    scaled = (floats * scaling[None, None, :, None]).astype(jnp.bfloat16)
    matches = bin_of_sample[:, None] == jnp.arange(TBINS, dtype=jnp.int32)[None, :]
    onehot = matches.astype(jnp.bfloat16)
    counts = jnp.sum(matches.astype(jnp.float32), axis=0)
    by_channel = jnp.moveaxis(scaled, 2, 0)
    weights_by = jnp.moveaxis(beam_weights, 1, 0)

    def one_channel(items):
        return channel_average(items[0], items[1], onehot, counts)

    averaged = lax.map(one_channel, (by_channel, weights_by))
    return averaged.reshape(CH, BEAMS * TBINS).astype(jnp.bfloat16)
```

```python
import functools

import jax
import jax.numpy as jnp
from jax import lax
from jax.experimental import pallas as pl
from jax.experimental.pallas import tpu as pltpu
from jax.sharding import PartitionSpec as P

TBINS = 64
LANES = 128
MESH = pl.DeviceIdType.MESH


def kernel(
    nd, nc, group,
    vt_ref, w_ref, flag_ref, width_ref, onehot_ref, count_ref,
    out_ref,
    volts, wbuf, qbuf, rbuf, stage,
    own_sem, w_sem, send1, recv1, send3, recv3, self_sem,
):
    channels = vt_ref.shape[1]
    groups = channels // group
    dishes = w_ref.shape[2]
    beams = w_ref.shape[3]
    samples = vt_ref.shape[4]
    devices = nd * nc
    pairs = beams // 2
    own_pairs = pairs // devices
    me_d = lax.axis_index("dish")
    me_c = lax.axis_index("chan")
    me = me_d * nc + me_c
    my_row = (me_c * nd + me_d) * channels

    def volt_copy(g, off):
        peer = lax.rem(me_d + off, nd)
        return pltpu.make_async_remote_copy(
            src_ref=vt_ref.at[peer, pl.ds(g * group, group)],
            dst_ref=volts.at[me_d, pl.ds(g * group, group)],
            send_sem=send1.at[g, off],
            recv_sem=recv1.at[g, off],
            device_id=(peer, me_c),
            device_id_type=MESH,
        )

    def volt_arrival(g, off):
        source = lax.rem(me_d + nd - off, nd)
        here = volts.at[source, pl.ds(g * group, group)]
        return pltpu.make_async_remote_copy(
            src_ref=here, dst_ref=here, send_sem=send1.at[g, off], recv_sem=recv1.at[g, off],
            device_id=(source, me_c), device_id_type=MESH,
        )

    def own_copy(g):
        return pltpu.make_async_copy(
            vt_ref.at[me_d, pl.ds(g * group, group)], volts.at[me_d, pl.ds(g * group, group)], own_sem.at[g]
        )

    def weight_copy(g):
        slot = lax.rem(g, 2)
        return pltpu.make_async_copy(w_ref.at[:, pl.ds(g * group, group)], wbuf.at[slot], w_sem.at[slot])

    def start_volts(g, _):
        for off in range(1, nd):
            volt_copy(g, off).start()
        own_copy(g).start()
        return 0

    lax.fori_loop(0, groups, start_volts, 0)
    weight_copy(0).start()

    def result_copy(g, off):
        target = lax.rem(me + off, devices)
        return pltpu.make_async_remote_copy(
            src_ref=stage.at[g, target],
            dst_ref=out_ref.at[pl.ds(pl.multiple_of(my_row + g * group, group), group)],
            send_sem=send3.at[off],
            recv_sem=recv3.at[off],
            device_id=(target // nc, lax.rem(target, nc)),
            device_id_type=MESH,
        )

    def self_copy(g):
        return pltpu.make_async_copy(
            stage.at[g, me],
            out_ref.at[pl.ds(pl.multiple_of(my_row + g * group, group), group)],
            self_sem.at[g],
        )

    lane = lax.broadcasted_iota(jnp.int32, (pairs, LANES), 1)
    total = float(dishes * samples)
    block = min(256, beams)

    def one_group(g, _):
        slot = lax.rem(g, 2)

        @pl.when(g + 1 < groups)
        def _():
            weight_copy(g + 1).start()

        own_copy(g).wait()
        for off in range(1, nd):
            volt_arrival(g, off).wait_recv()
        weight_copy(g).wait()

        def one_channel(i, _):
            c = g * group + i
            both = volts[:, c]
            real = both[:, 0].reshape(dishes, samples)
            imag = both[:, 1].reshape(dishes, samples)
            real32 = real.astype(jnp.float32)
            imag32 = imag.astype(jnp.float32)
            power = real32 * real32 + imag32 * imag32
            one = jnp.sum(jnp.sum(power, axis=0, keepdims=True), axis=1, keepdims=True) / total
            two = jnp.sum(jnp.sum(power * power, axis=0, keepdims=True), axis=1, keepdims=True) / total
            ratio = two / (one * one + 1e-06)
            excess = (total + 1.0) / (total - 1.0) * (ratio - 1.0) - 1.0
            width = width_ref[c]
            scaling = flag_ref[c] * width / (width + excess * excess)
            factor = scaling * scaling / count_ref[...]
            right = jnp.concatenate(
                [jnp.concatenate([real, imag], axis=1), jnp.concatenate([-imag, real], axis=1)], axis=0
            )
            for at in range(0, beams, block):
                left = jnp.concatenate(
                    [wbuf[slot, 0, i, :, pl.ds(at, block)], wbuf[slot, 1, i, :, pl.ds(at, block)]], axis=0
                )
                beam = lax.dot_general(
                    left, right, (((0,), (0,)), ((), ())), preferred_element_type=jnp.float32
                )
                re = beam[:, :samples]
                im = beam[:, samples:]
                detected = (re * re + im * im).astype(jnp.bfloat16)
                binned = jnp.dot(detected, onehot_ref[...], preferred_element_type=jnp.float32)
                qbuf[pl.ds(at, block), :] = binned * factor
            even = qbuf[pl.ds(0, pairs, stride=2), :]
            odd = qbuf[pl.ds(1, pairs, stride=2), :]
            rbuf[pl.ds(i, pairs, stride=group), :] = jnp.where(lane < TBINS, even, odd)
            return 0

        lax.fori_loop(0, group, one_channel, 0)

        def one_target(j, _):
            for p in range(own_pairs):
                row = pl.multiple_of((j * own_pairs + p) * group, group)
                stage[g, j, :, pl.ds(p * LANES, LANES)] = rbuf[pl.ds(row, group), :].astype(jnp.bfloat16)
            return 0

        lax.fori_loop(0, devices, one_target, 0)

        def send(off, _):
            result_copy(g, off).start()
            return 0

        lax.fori_loop(1, devices, send, 0)
        self_copy(g).start()
        return 0

    lax.fori_loop(0, groups, one_group, 0)

    def finish(g, _):
        for off in range(1, nd):
            volt_copy(g, off).wait_send()
        self_copy(g).wait()
        return 0

    lax.fori_loop(0, groups, finish, 0)

    def drain(off, _):
        source = lax.rem(me + devices - off, devices)
        row = (lax.rem(source, nc) * nd + source // nc) * channels
        block_ref = out_ref.at[pl.ds(pl.multiple_of(row, group), channels)]
        landed = pltpu.make_async_remote_copy(
            src_ref=block_ref, dst_ref=block_ref, send_sem=send3.at[off], recv_sem=recv3.at[off],
            device_id=(source // nc, lax.rem(source, nc)), device_id_type=MESH,
        )
        landed.wait_send()
        landed.wait_recv()
        return 0

    lax.fori_loop(1, devices, drain, 0)


def solution(mesh):
    nd, nc = mesh.shape["dish"], mesh.shape["chan"]

    def body(voltages, beam_weights, flags, sk_bins, bin_of_sample):
        _, local_dishes, block_channels, samples = voltages.shape
        _, channels, dishes, beams = beam_weights.shape
        devices = nd * nc
        group = min(16, channels)
        groups = channels // group
        columns = beams // devices * TBINS
        vt = jnp.transpose(voltages, (2, 0, 1, 3)).reshape(nd, channels, 2, local_dishes, samples)
        start = lax.axis_index("dish") * channels
        spread = lambda x: jnp.broadcast_to(
            lax.dynamic_slice(x, (start,), (channels,)).astype(jnp.float32)[:, None, None], (channels, 1, LANES)
        )
        bins = jnp.arange(LANES, dtype=jnp.int32) % TBINS
        matches = bin_of_sample[:, None] == bins[None, :]
        onehot = matches.astype(jnp.bfloat16)
        counts = jnp.sum(matches.astype(jnp.float32), axis=0, keepdims=True)
        anywhere = pl.BlockSpec(memory_space=pl.ANY)
        local = pl.BlockSpec(memory_space=pltpu.VMEM)
        return pl.pallas_call(
            functools.partial(kernel, nd, nc, group),
            out_shape=jax.ShapeDtypeStruct((devices * channels, columns), jnp.bfloat16),
            in_specs=[anywhere, anywhere, local, local, local, local],
            out_specs=anywhere,
            scratch_shapes=[
                pltpu.VMEM((nd, channels, 2, local_dishes, samples), jnp.bfloat16),
                pltpu.VMEM((2, 2, group, dishes, beams), jnp.bfloat16),
                pltpu.VMEM((beams, LANES), jnp.float32),
                pltpu.VMEM((beams // 2 * group, LANES), jnp.float32),
                pltpu.VMEM((groups, devices, group, columns), jnp.bfloat16),
                pltpu.SemaphoreType.DMA((groups,)),
                pltpu.SemaphoreType.DMA((2,)),
                pltpu.SemaphoreType.DMA((groups, nd)),
                pltpu.SemaphoreType.DMA((groups, nd)),
                pltpu.SemaphoreType.DMA((devices,)),
                pltpu.SemaphoreType.DMA((devices,)),
                pltpu.SemaphoreType.DMA((groups,)),
            ],
            compiler_params=pltpu.CompilerParams(has_side_effects=True, vmem_limit_bytes=62 * 1024 * 1024),
        )(vt, beam_weights, spread(flags), 0.05 * spread(sk_bins), onehot, counts)

    in_specs = (
        P(None, "dish", "chan", None),
        P(None, ("chan", "dish"), None, None),
        P("chan"),
        P("chan"),
        P(),
    )
    return jax.shard_map(
        body, mesh=mesh, in_specs=in_specs, out_specs=P(None, ("dish", "chan")), check_vma=False
    )
```

```python
import functools

import jax
import jax.numpy as jnp
from jax import lax
from jax.experimental import pallas as pl
from jax.experimental.pallas import tpu as pltpu
from jax.sharding import PartitionSpec as P

TBINS = 64
LANES = 128
MESH = pl.DeviceIdType.MESH


def kernel(
    nd, nc, group,
    v_ref, w_ref, flag_ref, sk_ref, bin_ref,
    out_ref,
    volts, fbuf, wbuf, qbuf, rbuf, stage, onehot, counts,
    own_sem, w_sem, send1, recv1, send3, recv3, self_sem,
):
    channels = w_ref.shape[1]
    local_dishes = v_ref.shape[1]
    groups = channels // group
    dishes = w_ref.shape[2]
    beams = w_ref.shape[3]
    samples = v_ref.shape[3]
    devices = nd * nc
    pairs = beams // 2
    own_pairs = pairs // devices
    me_d = lax.axis_index("dish")
    me_c = lax.axis_index("chan")
    me = me_d * nc + me_c
    my_row = (me_c * nd + me_d) * channels

    def volt_copy(g, off):
        peer = lax.rem(me_d + off, nd)
        return pltpu.make_async_remote_copy(
            src_ref=v_ref.at[:, :, pl.ds(pl.multiple_of(peer * channels + g * group, group), group)],
            dst_ref=volts.at[g, me_d],
            send_sem=send1.at[g, off],
            recv_sem=recv1.at[g, off],
            device_id=(peer, me_c),
            device_id_type=MESH,
        )

    def volt_arrival(g, off):
        source = lax.rem(me_d + nd - off, nd)
        here = volts.at[g, source]
        return pltpu.make_async_remote_copy(
            src_ref=here, dst_ref=here, send_sem=send1.at[g, off], recv_sem=recv1.at[g, off],
            device_id=(source, me_c), device_id_type=MESH,
        )

    def own_copy(g):
        return pltpu.make_async_copy(
            v_ref.at[:, :, pl.ds(pl.multiple_of(me_d * channels + g * group, group), group)],
            volts.at[g, me_d],
            own_sem.at[g],
        )

    def weight_copy(g):
        slot = lax.rem(g, 2)
        return pltpu.make_async_copy(w_ref.at[:, pl.ds(g * group, group)], wbuf.at[slot], w_sem.at[slot])

    def start_volts(g, _):
        for off in range(1, nd):
            volt_copy(g, off).start()
        own_copy(g).start()
        return 0

    lax.fori_loop(0, groups, start_volts, 0)
    weight_copy(0).start()

    bins = lax.rem(lax.broadcasted_iota(jnp.int32, (LANES, samples), 0), TBINS)
    matches = jnp.where(bin_ref[...] == bins, 1.0, 0.0).astype(jnp.float32)
    turned = matches.T
    onehot[...] = turned.astype(jnp.bfloat16)
    counts[...] = jnp.sum(turned, axis=0, keepdims=True)

    def result_copy(g, off):
        target = lax.rem(me + off, devices)
        return pltpu.make_async_remote_copy(
            src_ref=stage.at[g, target],
            dst_ref=out_ref.at[pl.ds(pl.multiple_of(my_row + g * group, group), group)],
            send_sem=send3.at[off],
            recv_sem=recv3.at[off],
            device_id=(target // nc, lax.rem(target, nc)),
            device_id_type=MESH,
        )

    def self_copy(g):
        return pltpu.make_async_copy(
            stage.at[g, me],
            out_ref.at[pl.ds(pl.multiple_of(my_row + g * group, group), group)],
            self_sem.at[g],
        )

    lane = lax.broadcasted_iota(jnp.int32, (pairs, LANES), 1)
    total = float(dishes * samples)
    block = min(256, beams)

    def one_group(g, _):
        slot = lax.rem(g, 2)

        @pl.when(g + 1 < groups)
        def _():
            weight_copy(g + 1).start()

        own_copy(g).wait()
        for off in range(1, nd):
            volt_arrival(g, off).wait_recv()
        weight_copy(g).wait()

        for part in range(2):
            for source in range(nd):
                rows = local_dishes * group
                wide = volts[g, source, part].astype(jnp.float32).reshape(rows, samples)
                for t in range(samples // LANES):
                    fbuf[t, pl.ds((part * nd + source) * rows, rows), :] = wide[:, t * LANES : (t + 1) * LANES]

        def one_channel(i, _):
            c = me_d * channels + g * group + i
            spots = range(samples // LANES)
            real32 = jnp.concatenate([fbuf[t, pl.ds(i, dishes, stride=group), :] for t in spots], axis=1)
            imag32 = jnp.concatenate(
                [fbuf[t, pl.ds(dishes * group + i, dishes, stride=group), :] for t in spots], axis=1
            )
            real = real32.astype(jnp.bfloat16)
            imag = imag32.astype(jnp.bfloat16)
            power = real32 * real32 + imag32 * imag32
            one = jnp.sum(jnp.sum(power, axis=0, keepdims=True), axis=1, keepdims=True) / total
            two = jnp.sum(jnp.sum(power * power, axis=0, keepdims=True), axis=1, keepdims=True) / total
            ratio = two / (one * one + 1e-06)
            excess = (total + 1.0) / (total - 1.0) * (ratio - 1.0) - 1.0
            width = 0.05 * sk_ref[c].astype(jnp.float32)
            scaling = flag_ref[c].astype(jnp.float32) * width / (width + excess * excess)
            factor = scaling * scaling / counts[...]
            right = jnp.concatenate(
                [jnp.concatenate([real, imag], axis=1), jnp.concatenate([-imag, real], axis=1)], axis=0
            )
            for at in range(0, beams, block):
                left = jnp.concatenate(
                    [wbuf[slot, 0, i, :, pl.ds(at, block)], wbuf[slot, 1, i, :, pl.ds(at, block)]], axis=0
                )
                beam = lax.dot_general(
                    left, right, (((0,), (0,)), ((), ())), preferred_element_type=jnp.float32
                )
                re = beam[:, :samples]
                im = beam[:, samples:]
                detected = (re * re + im * im).astype(jnp.bfloat16)
                binned = jnp.dot(detected, onehot[...], preferred_element_type=jnp.float32)
                qbuf[pl.ds(at, block), :] = binned * factor
            even = qbuf[pl.ds(0, pairs, stride=2), :]
            odd = qbuf[pl.ds(1, pairs, stride=2), :]
            rbuf[pl.ds(i, pairs, stride=group), :] = jnp.where(lane < TBINS, even, odd)
            return 0

        lax.fori_loop(0, group, one_channel, 0)

        def one_target(j, _):
            for p in range(own_pairs):
                row = pl.multiple_of((j * own_pairs + p) * group, group)
                stage[g, j, :, pl.ds(p * LANES, LANES)] = rbuf[pl.ds(row, group), :].astype(jnp.bfloat16)
            return 0

        lax.fori_loop(0, devices, one_target, 0)

        def send(off, _):
            result_copy(g, off).start()
            return 0

        lax.fori_loop(1, devices, send, 0)
        self_copy(g).start()
        return 0

    lax.fori_loop(0, groups, one_group, 0)

    def finish(g, _):
        for off in range(1, nd):
            volt_copy(g, off).wait_send()
        self_copy(g).wait()
        return 0

    lax.fori_loop(0, groups, finish, 0)

    def drain(off, _):
        source = lax.rem(me + devices - off, devices)
        row = (lax.rem(source, nc) * nd + source // nc) * channels
        block_ref = out_ref.at[pl.ds(pl.multiple_of(row, group), channels)]
        landed = pltpu.make_async_remote_copy(
            src_ref=block_ref, dst_ref=block_ref, send_sem=send3.at[off], recv_sem=recv3.at[off],
            device_id=(source // nc, lax.rem(source, nc)), device_id_type=MESH,
        )
        landed.wait_send()
        landed.wait_recv()
        return 0

    lax.fori_loop(1, devices, drain, 0)


def solution(mesh):
    nd, nc = mesh.shape["dish"], mesh.shape["chan"]

    def body(voltages, beam_weights, flags, sk_bins, bin_of_sample):
        _, local_dishes, _, samples = voltages.shape
        _, channels, dishes, beams = beam_weights.shape
        devices = nd * nc
        group = min(8, channels)
        groups = channels // group
        columns = beams // devices * TBINS
        anywhere = pl.BlockSpec(memory_space=pl.ANY)
        local = pl.BlockSpec(memory_space=pltpu.VMEM)
        scalars = pl.BlockSpec(memory_space=pltpu.SMEM)
        return pl.pallas_call(
            functools.partial(kernel, nd, nc, group),
            out_shape=jax.ShapeDtypeStruct((devices * channels, columns), jnp.bfloat16),
            in_specs=[anywhere, anywhere, scalars, scalars, local],
            out_specs=anywhere,
            scratch_shapes=[
                pltpu.VMEM((groups, nd, 2, local_dishes, group, samples), jnp.bfloat16),
                pltpu.VMEM((samples // LANES, 2 * dishes * group, LANES), jnp.float32),
                pltpu.VMEM((2, 2, group, dishes, beams), jnp.bfloat16),
                pltpu.VMEM((beams, LANES), jnp.float32),
                pltpu.VMEM((beams // 2 * group, LANES), jnp.float32),
                pltpu.VMEM((groups, devices, group, columns), jnp.bfloat16),
                pltpu.VMEM((samples, LANES), jnp.bfloat16),
                pltpu.VMEM((1, LANES), jnp.float32),
                pltpu.SemaphoreType.DMA((groups,)),
                pltpu.SemaphoreType.DMA((2,)),
                pltpu.SemaphoreType.DMA((groups, nd)),
                pltpu.SemaphoreType.DMA((groups, nd)),
                pltpu.SemaphoreType.DMA((devices,)),
                pltpu.SemaphoreType.DMA((devices,)),
                pltpu.SemaphoreType.DMA((groups,)),
            ],
            compiler_params=pltpu.CompilerParams(has_side_effects=True, vmem_limit_bytes=62 * 1024 * 1024),
        )(voltages, beam_weights, flags, sk_bins, bin_of_sample.reshape(1, samples))

    in_specs = (
        P(None, "dish", "chan", None),
        P(None, ("chan", "dish"), None, None),
        P("chan"),
        P("chan"),
        P(),
    )
    return jax.shard_map(
        body, mesh=mesh, in_specs=in_specs, out_specs=P(None, ("dish", "chan")), check_vma=False
    )
```

```python
import functools

import jax
import jax.numpy as jnp
from jax import lax
from jax.experimental import pallas as pl
from jax.experimental.pallas import tpu as pltpu
from jax.sharding import PartitionSpec as P

TBINS = 64
LANES = 128
MESH = pl.DeviceIdType.MESH


def kernel(
    nd, nc, group,
    v_ref, w_ref, flag_ref, sk_ref, bin_ref,
    out_ref,
    volts, fbuf, wbuf, qbuf, rbuf, stage, onehot, counts,
    own_sem, w_sem, send1, recv1, send3, recv3, self_sem,
):
    channels = w_ref.shape[1]
    local_dishes = v_ref.shape[1]
    groups = channels // group
    dishes = w_ref.shape[2]
    beams = w_ref.shape[3]
    samples = v_ref.shape[3]
    devices = nd * nc
    pairs = beams // 2
    own_pairs = pairs // devices
    me_d = lax.axis_index("dish")
    me_c = lax.axis_index("chan")
    me = me_d * nc + me_c
    my_row = (me_c * nd + me_d) * channels

    def volt_copy(g, off):
        peer = lax.rem(me_d + off, nd)
        return pltpu.make_async_remote_copy(
            src_ref=v_ref.at[:, :, pl.ds(pl.multiple_of(peer * channels + g * group, group), group)],
            dst_ref=volts.at[g, me_d],
            send_sem=send1.at[g, off],
            recv_sem=recv1.at[g, off],
            device_id=(peer, me_c),
            device_id_type=MESH,
        )

    def volt_arrival(g, off):
        source = lax.rem(me_d + nd - off, nd)
        here = volts.at[g, source]
        return pltpu.make_async_remote_copy(
            src_ref=here, dst_ref=here, send_sem=send1.at[g, off], recv_sem=recv1.at[g, off],
            device_id=(source, me_c), device_id_type=MESH,
        )

    def own_copy(g):
        return pltpu.make_async_copy(
            v_ref.at[:, :, pl.ds(pl.multiple_of(me_d * channels + g * group, group), group)],
            volts.at[g, me_d],
            own_sem.at[g],
        )

    def weight_copy(g):
        slot = lax.rem(g, 2)
        return pltpu.make_async_copy(w_ref.at[:, pl.ds(g * group, group)], wbuf.at[slot], w_sem.at[slot])

    def start_volts(g, _):
        for off in range(1, nd):
            volt_copy(g, off).start()
        own_copy(g).start()
        return 0

    lax.fori_loop(0, groups, start_volts, 0)
    weight_copy(0).start()

    bins = lax.rem(lax.broadcasted_iota(jnp.int32, (LANES, samples), 0), TBINS)
    matches = jnp.where(bin_ref[...] == bins, 1.0, 0.0).astype(jnp.float32)
    turned = matches.T
    onehot[...] = turned.astype(jnp.bfloat16)
    counts[...] = jnp.sum(turned, axis=0, keepdims=True)

    def result_copy(g, off, target):
        return pltpu.make_async_remote_copy(
            src_ref=stage.at[g, target],
            dst_ref=out_ref.at[pl.ds(pl.multiple_of(my_row + g * group, group), group)],
            send_sem=send3.at[off],
            recv_sem=recv3.at[off],
            device_id=(target // nc, lax.rem(target, nc)),
            device_id_type=MESH,
        )

    def self_copy(g):
        return pltpu.make_async_copy(
            stage.at[g, me],
            out_ref.at[pl.ds(pl.multiple_of(my_row + g * group, group), group)],
            self_sem.at[g],
        )

    lane = lax.broadcasted_iota(jnp.int32, (min(256, beams) // 2, LANES), 1)
    total = float(dishes * samples)
    block = min(256, beams)

    def prepare(g):
        @pl.when(g + 1 < groups)
        def _():
            weight_copy(g + 1).start()

        own_copy(g).wait()
        for off in range(1, nd):
            volt_arrival(g, off).wait_recv()
        weight_copy(g).wait()

        for part in range(2):
            for source in range(nd):
                rows = local_dishes * group
                wide = volts[g, source, part].astype(jnp.float32).reshape(rows, samples)
                for t in range(samples // LANES):
                    fbuf[t, pl.ds((part * nd + source) * rows, rows), :] = wide[:, t * LANES : (t + 1) * LANES]

    def work(g, first, count):
        slot = lax.rem(g, 2)
        parts = beams // block
        half = block // 2

        def one_channel(i, _):
            c = me_d * channels + g * group + i
            spots = range(samples // LANES)
            real32 = jnp.concatenate([fbuf[t, pl.ds(i, dishes, stride=group), :] for t in spots], axis=1)
            imag32 = jnp.concatenate(
                [fbuf[t, pl.ds(dishes * group + i, dishes, stride=group), :] for t in spots], axis=1
            )
            real = real32.astype(jnp.bfloat16)
            imag = imag32.astype(jnp.bfloat16)
            power = real32 * real32 + imag32 * imag32
            one = jnp.sum(jnp.sum(power, axis=0, keepdims=True), axis=1, keepdims=True) / total
            two = jnp.sum(jnp.sum(power * power, axis=0, keepdims=True), axis=1, keepdims=True) / total
            ratio = two / (one * one + 1e-06)
            excess = (total + 1.0) / (total - 1.0) * (ratio - 1.0) - 1.0
            width = 0.05 * sk_ref[c].astype(jnp.float32)
            scaling = flag_ref[c].astype(jnp.float32) * width / (width + excess * excess)
            factor = scaling * scaling / counts[...]
            right = jnp.concatenate(
                [jnp.concatenate([real, imag], axis=1), jnp.concatenate([-imag, real], axis=1)], axis=0
            )
            for n in range(count):
                at = pl.multiple_of((first + n) * block, block)
                left = jnp.concatenate(
                    [wbuf[slot, 0, i, :, pl.ds(at, block)], wbuf[slot, 1, i, :, pl.ds(at, block)]], axis=0
                )
                beam = lax.dot_general(
                    left, right, (((0,), (0,)), ((), ())), preferred_element_type=jnp.float32
                )
                re = beam[:, :samples]
                im = beam[:, samples:]
                detected = (re * re + im * im).astype(jnp.bfloat16)
                binned = jnp.dot(detected, onehot[...], preferred_element_type=jnp.float32)
                qbuf[pl.ds(n * block, block), :] = binned * factor
                even = qbuf[pl.ds(n * block, half, stride=2), :]
                odd = qbuf[pl.ds(n * block + 1, half, stride=2), :]
                rbuf[pl.ds((first + n) * half * group + i, half, stride=group), :] = jnp.where(
                    lane < TBINS, even, odd
                )
            return 0

        lax.fori_loop(0, group, one_channel, 0)
        low = first * (devices // parts)
        served = count * (devices // parts)

        def one_target(j, _):
            for p in range(own_pairs):
                row = pl.multiple_of((j * own_pairs + p) * group, group)
                stage[g, j, :, pl.ds(p * LANES, LANES)] = rbuf[pl.ds(row, group), :].astype(jnp.bfloat16)
            return 0

        lax.fori_loop(low, low + served, one_target, 0)

        def send(k, _):
            target = low + lax.rem(me + 1 + k, served)
            off = lax.rem(target - me + devices, devices)

            @pl.when(off != 0)
            def _():
                result_copy(g, off, target).start()

            @pl.when(off == 0)
            def _():
                self_copy(g).start()

            return 0

        lax.fori_loop(0, served, send, 0)

    parts = beams // block
    prepare(0)

    def one_part(b, _):
        work(0, lax.rem(me_d + b, parts), 1)
        return 0

    lax.fori_loop(0, parts, one_part, 0)

    def one_group(g, _):
        prepare(g)
        work(g, 0, parts)
        return 0

    lax.fori_loop(1, groups, one_group, 0)

    def finish(g, _):
        for off in range(1, nd):
            volt_copy(g, off).wait_send()
        self_copy(g).wait()
        return 0

    lax.fori_loop(0, groups, finish, 0)

    def drain(off, _):
        source = lax.rem(me + devices - off, devices)
        row = (lax.rem(source, nc) * nd + source // nc) * channels
        block_ref = out_ref.at[pl.ds(pl.multiple_of(row, group), channels)]
        landed = pltpu.make_async_remote_copy(
            src_ref=block_ref, dst_ref=block_ref, send_sem=send3.at[off], recv_sem=recv3.at[off],
            device_id=(source // nc, lax.rem(source, nc)), device_id_type=MESH,
        )
        landed.wait_send()
        landed.wait_recv()
        return 0

    lax.fori_loop(1, devices, drain, 0)


def solution(mesh):
    nd, nc = mesh.shape["dish"], mesh.shape["chan"]

    def body(voltages, beam_weights, flags, sk_bins, bin_of_sample):
        _, local_dishes, _, samples = voltages.shape
        _, channels, dishes, beams = beam_weights.shape
        devices = nd * nc
        group = min(8, channels)
        groups = channels // group
        columns = beams // devices * TBINS
        anywhere = pl.BlockSpec(memory_space=pl.ANY)
        local = pl.BlockSpec(memory_space=pltpu.VMEM)
        scalars = pl.BlockSpec(memory_space=pltpu.SMEM)
        return pl.pallas_call(
            functools.partial(kernel, nd, nc, group),
            out_shape=pltpu.VMEM((devices * channels, columns), jnp.bfloat16),
            in_specs=[anywhere, anywhere, scalars, scalars, local],
            out_specs=local,
            scratch_shapes=[
                pltpu.VMEM((groups, nd, 2, local_dishes, group, samples), jnp.bfloat16),
                pltpu.VMEM((samples // LANES, 2 * dishes * group, LANES), jnp.float32),
                pltpu.VMEM((2, 2, group, dishes, beams), jnp.bfloat16),
                pltpu.VMEM((beams, LANES), jnp.float32),
                pltpu.VMEM((beams // 2 * group, LANES), jnp.float32),
                pltpu.VMEM((groups, devices, group, columns), jnp.bfloat16),
                pltpu.VMEM((samples, LANES), jnp.bfloat16),
                pltpu.VMEM((1, LANES), jnp.float32),
                pltpu.SemaphoreType.DMA((groups,)),
                pltpu.SemaphoreType.DMA((2,)),
                pltpu.SemaphoreType.DMA((groups, nd)),
                pltpu.SemaphoreType.DMA((groups, nd)),
                pltpu.SemaphoreType.DMA((devices,)),
                pltpu.SemaphoreType.DMA((devices,)),
                pltpu.SemaphoreType.DMA((groups,)),
            ],
            compiler_params=pltpu.CompilerParams(has_side_effects=True, vmem_limit_bytes=46 * 1024 * 1024),
        )(voltages, beam_weights, flags, sk_bins, bin_of_sample.reshape(1, samples))

    in_specs = (
        P(None, "dish", "chan", None),
        P(None, ("chan", "dish"), None, None),
        P("chan"),
        P("chan"),
        P(),
    )
    return jax.shard_map(
        body, mesh=mesh, in_specs=in_specs, out_specs=P(None, ("dish", "chan")), check_vma=False
    )
```
